32 devices in a mesh: col: 16 (over z, y, x), grp: 2 (over core).
Axes of the slice: x: 2, y: 2, z: 4, core: 2. Of those that a mesh axis runs over, the one named last changes fastest.
Arguments:
- diag_blocks: float32 [16, 128, 128], P('col'), as said below
- panel_blocks: float32 [16, 2, 128, 128], P('col', 'grp'), as said below
- targets: int32 [16, 2], replicated, may hold values from 0 to 16, as said below
Outputs:
- factor_diag: float32 [16, 128, 128], P('col')
- factor_panel: float32 [16, 2, 128, 128], P('col', 'grp')
The draws below stay inside these ranges and needn't reach their ends.
Inputs may be any that keep to these rules, and one draw needn't show every extreme that they name: targets[s, 0] is the parent of supernode s and targets[s, 1] = targets[targets[s, 0], 0] its grandparent, 16 where that ancestor lies outside the window; the tree is a binary heap under a random labelling: exactly one root, every supernode has at most two children and at most four grandchildren, and level d holds min(2 ** d, 16 - 2 ** d + 1) supernodes. `diag_blocks`: each block is symmetric positive definite, and every updated diagonal block stays positive definite. `panel_blocks`: every entry lies within 8 / sqrt(128) of zero.
All inputs are finite; a program needn't handle non-finite values.
Results may differ from the reference program's by a relative error of at most 0.00095.
Values may be sent and summed in bfloat16 or wider, within the bound.
A program may use at most 64 MiB of HBM per device.

```python
import jax
import jax.numpy as jnp
from jax import lax

W = 128
NS = 16


def draw_targets(key, part):
    heap_pos = jax.random.permutation(key, NS).astype(jnp.int32)
    labels = jnp.argsort(heap_pos).astype(jnp.int32)
    above = jnp.maximum(heap_pos - 1, 0) // 2
    parent = jnp.where(heap_pos > 0, labels[above], NS).astype(jnp.int32)
    extended = jnp.concatenate([parent, jnp.array([NS], jnp.int32)])
    grand = extended[parent]
    return jnp.stack([parent, grand], 1).astype(jnp.int32)


def draw_diag_blocks(key, part):
    noise_key = jax.random.fold_in(key, 11)
    level_key = jax.random.fold_in(key, 23)
    noise = jax.random.normal(noise_key, (NS, W, W), jnp.float32)
    levels = 8.0 + 8.0 * jax.random.uniform(level_key, (NS, W), jnp.float32)
    symmetric = (noise + jnp.swapaxes(noise, 1, 2)) * (1.0 / 2.0 ** 0.5 / W ** 0.5)
    return (symmetric + levels[:, :, None] * jnp.eye(W, dtype=jnp.float32)[None]).astype(jnp.float32)


def draw_panel_blocks(key, part):
    entry_key = jax.random.fold_in(key, 37)
    spread = 1.8 / W ** 0.5
    values = jnp.clip(jax.random.normal(entry_key, (NS, 2, W, W), jnp.float32), -4.0, 4.0)
    return (values * spread).astype(jnp.float32)


def setup_inputs(seed: int = 0) -> dict:
    arg_keys = jax.random.split(jax.random.key(seed), 4)
    diag_blocks = draw_diag_blocks(jax.random.fold_in(arg_keys[3], 71), 0)
    panel_blocks = draw_panel_blocks(jax.random.fold_in(arg_keys[3], 71), 0)
    targets = draw_targets(jax.random.fold_in(arg_keys[3], 71), 0)
    return {"diag_blocks": diag_blocks, "panel_blocks": panel_blocks, "targets": targets}


def node_depth(parent, nodes):
    extended = jnp.concatenate([parent, jnp.array([nodes], jnp.int32)])
    depth = jnp.zeros((nodes,), jnp.int32)
    current = parent
    for index in range(nodes.bit_length()):
        depth = depth + (current < nodes).astype(jnp.int32)
        current = extended[current]
    return depth

def solve_right(lower, panel):

    def one(factor, block):
        return jax.scipy.linalg.solve_triangular(factor, block.T, lower=True).T
    return jax.vmap(one)(lower, panel)

def rounded(values):
    low = values.astype(jnp.bfloat16)
    low = lax.optimization_barrier(low)
    return low.astype(jnp.float32)

def reference(diag_blocks, panel_blocks, targets):
    parent = targets[:, 0]
    grand = targets[:, 1]
    depth = node_depth(parent, NS)
    acc_diag = diag_blocks
    acc_near = panel_blocks[:, 0]
    far_panel = panel_blocks[:, 1]
    out_diag = jnp.zeros_like(diag_blocks)
    output_panel = jnp.zeros_like(panel_blocks)
    for level in range(NS.bit_length() - 1, -1, -1):
        active_nodes = depth == level
        wide_mask = active_nodes[:, None, None]
        lower = jnp.linalg.cholesky(acc_diag)
        near = solve_right(lower, acc_near)
        far = solve_right(lower, far_panel)
        out_diag = jnp.where(wide_mask, lower, out_diag)
        output_panel = jnp.where(wide_mask[:, None], jnp.stack([near, far], 1), output_panel)
        if level > 0:
            near_low = rounded(jnp.where(wide_mask, near, 0.0))
            far_low = rounded(jnp.where(wide_mask, far, 0.0))
            diag_near = jnp.einsum('cab,cdb->cad', near_low, near_low, precision=lax.Precision.HIGHEST)
            diag_far = jnp.einsum('cab,cdb->cad', far_low, far_low, precision=lax.Precision.HIGHEST)
            cross_far = jnp.einsum('cab,cdb->cad', far_low, near_low, precision=lax.Precision.HIGHEST)
            seg_near = jnp.where(active_nodes, parent, NS)
            seg_far = jnp.where(active_nodes, grand, NS)
            acc_diag = acc_diag - jax.ops.segment_sum(diag_near, seg_near, NS + 1)[:NS]
            acc_diag = acc_diag - jax.ops.segment_sum(diag_far, seg_far, NS + 1)[:NS]
            acc_near = acc_near - jax.ops.segment_sum(cross_far, seg_near, NS + 1)[:NS]
    return (out_diag, output_panel)
```

```python
import functools

import jax
import jax.numpy as jnp
from jax import lax
from jax.experimental import pallas as pl
from jax.experimental.pallas import tpu as pltpu
from jax.sharding import PartitionSpec as P

MESH = pl.DeviceIdType.MESH
BLOCK = 16
HIGHEST = lax.Precision.HIGHEST


def across(value, width):
    return jnp.broadcast_to(value, (value.shape[0], width))


def factor_rows(work, width):
    total = 2 * width
    for first in range(0, width, BLOCK):
        rows = work[first:first + BLOCK, :]
        columns = [across(rows[:, first + j:first + j + 1], 128) for j in range(BLOCK)]
        index = lax.broadcasted_iota(jnp.int32, (BLOCK, 128), 0)
        done = []
        for j in range(BLOCK):
            pivot = columns[j][j:j + 1, :]
            inverse = lax.rsqrt(pivot)
            scaled = columns[j] * inverse
            below = jnp.where(index > j, scaled, 0.0)
            for k in range(j + 1, BLOCK):
                entry = scaled[k:k + 1, :]
                columns[k] = columns[k] - below * entry
            lead = [rows[j:j + 1, h:h + 128] * inverse for h in range(0, total, 128)]
            lead = jnp.concatenate(lead, 1)
            done.append(lead)
            if j + 1 < BLOCK:
                wide = jnp.concatenate([below] * (total // 128), 1)
                rows = rows - wide * lead
        upper = jnp.concatenate(done, 0)
        work[first:first + BLOCK, :] = upper
        if first + BLOCK < width:
            left = upper[:, :width]
            change = lax.dot_general(left, upper, (((0,), (0,)), ((), ())),
                                     precision=HIGHEST, preferred_element_type=jnp.float32)
            work[first + BLOCK:, :] = work[first + BLOCK:, :] - change[first + BLOCK:, :]


def kernel(nodes, levels, targets, diag, panel, out_diag, out_panel, acc, work, part,
           got_part, kids_out, kids_in, send_sem, recv_sem, pair_send, pair_recv, *slots):
    width = diag.shape[-1]
    me = lax.axis_index("col")
    core = lax.axis_index("grp")

    barrier = pltpu.get_barrier_semaphore()

    def greet(offset, carry):
        peer = lax.rem(me + offset, nodes)
        pl.semaphore_signal(barrier, inc=1, device_id=(peer, core), device_id_type=MESH)
        return carry

    lax.fori_loop(1, nodes, greet, 0)
    pl.semaphore_signal(barrier, inc=1, device_id=(me, 1 - core), device_id_type=MESH)

    acc[:, :width] = diag[...]
    acc[:, width:] = panel[...].T

    def parent_of(node):
        return jnp.where(node < nodes, targets[jnp.minimum(node, nodes - 1), 0], nodes)

    depth = jnp.int32(0)
    current = targets[me, 0]
    for _ in range(levels - 1):
        depth = depth + (current < nodes).astype(jnp.int32)
        current = parent_of(current)

    def search(node, carry):
        kid = targets[node, 0] == me
        grand = targets[node, 1] == me
        k0, k1, kc, g0, g1, g2, g3, gc = carry
        k0 = jnp.where(kid & (kc == 0), node, k0)
        k1 = jnp.where(kid & (kc == 1), node, k1)
        kc = kc + kid.astype(jnp.int32)
        g0 = jnp.where(grand & (gc == 0), node, g0)
        g1 = jnp.where(grand & (gc == 1), node, g1)
        g2 = jnp.where(grand & (gc == 2), node, g2)
        g3 = jnp.where(grand & (gc == 3), node, g3)
        gc = gc + grand.astype(jnp.int32)
        return k0, k1, kc, g0, g1, g2, g3, gc

    zero = jnp.int32(0)
    k0, k1, kc, g0, g1, g2, g3, gc = lax.fori_loop(0, nodes, search, (zero,) * 8)
    near_core = core == 0
    picks = [jnp.where(near_core, k0, g0), jnp.where(near_core, k1, g1), g2, g3]
    own_count = jnp.where(near_core, kc, gc)
    own_apart = jnp.where(near_core, 1, 2)

    pl.semaphore_wait(barrier, nodes)

    def pick(held, node, wanted):
        rows = held[node]
        return jnp.where(wanted, rows, jnp.zeros_like(rows))

    def send(step, held, solved):
        held[me] = solved.astype(jnp.bfloat16)

        def start(offset, carry):
            peer = lax.rem(me + offset, nodes)
            pltpu.make_async_remote_copy(
                src_ref=held.at[me], dst_ref=held.at[me],
                send_sem=send_sem.at[step], recv_sem=recv_sem.at[step],
                device_id=(peer, core), device_id_type=MESH).start()
            return carry

        lax.fori_loop(1, nodes, start, 0)

    def gather(step, held):
        level = levels - 1 - step
        everyone = held.at[pl.ds(0, nodes - 1)]
        pltpu.make_async_copy(everyone, everyone, recv_sem.at[step]).wait()
        is_kid = depth + 1 == level
        kid_a = pick(held, k0, is_kid & (kc > 0))
        kid_b = pick(held, k1, is_kid & (kc > 1))
        kids_out[step, :, :width] = kid_a
        kids_out[step, :, width:] = kid_b
        rows_copy = pltpu.make_async_remote_copy(
            src_ref=kids_out.at[step], dst_ref=kids_in.at[step],
            send_sem=pair_send.at[step, 0], recv_sem=pair_recv.at[step, 0],
            device_id=(me, 1 - core), device_id_type=MESH)
        rows_copy.start()
        mine = depth + own_apart == level
        four = [pick(held, picks[0], mine & (own_count > 0)),
                pick(held, picks[1], mine & (own_count > 1)),
                pick(held, picks[2], mine & (own_count > 2)),
                pick(held, picks[3], mine & (own_count > 3))]
        four = jnp.concatenate(four, 1)
        own = lax.dot_general(four, four, (((1,), (1,)), ((), ())),
                              preferred_element_type=jnp.float32)
        part[step] = own
        part_copy = pltpu.make_async_remote_copy(
            src_ref=part.at[step], dst_ref=got_part.at[step],
            send_sem=pair_send.at[step, 1], recv_sem=pair_recv.at[step, 1],
            device_id=(me, 1 - core), device_id_type=MESH)
        part_copy.start()
        rows_copy.wait()
        kids = jnp.concatenate([kid_a, kid_b], 1)
        cross = lax.dot_general(kids, kids_in[step], (((1,), (1,)), ((), ())),
                                preferred_element_type=jnp.float32)
        acc[:, width:] = acc[:, width:] - jnp.where(near_core, cross, 0.0)
        part_copy.wait()
        acc[:, :width] = acc[:, :width] - (own + got_part[step])
        pltpu.make_async_copy(everyone, everyone, send_sem.at[step]).wait()

    def level_step(step, carry):
        level = levels - 1 - step
        work[...] = acc[...]
        factor_rows(work, width)
        solved = work[:, width:].T
        active = depth == level

        for turn in range(levels - 1):
            pl.when(step == turn)(functools.partial(send, turn, slots[turn], solved))

        tri = lax.broadcasted_iota(jnp.int32, (width, width), 0)
        tri = tri >= lax.broadcasted_iota(jnp.int32, (width, width), 1)
        lower = jnp.where(tri, work[:, :width].T, 0.0)
        out_diag[...] = jnp.where(active, lower, out_diag[...])
        out_panel[...] = jnp.where(active, solved, out_panel[...])

        for turn in range(levels - 1):
            pl.when(step == turn)(functools.partial(gather, turn, slots[turn]))

        return carry

    out_diag[...] = jnp.zeros_like(out_diag)
    out_panel[...] = jnp.zeros_like(out_panel)
    lax.fori_loop(0, levels, level_step, 0)


def shards(diag_blocks, panel_blocks, targets):
    width = diag_blocks.shape[1]
    nodes = targets.shape[0]
    levels = nodes.bit_length()
    steps = levels - 1
    vmem = pl.BlockSpec(memory_space=pltpu.VMEM)
    dma = pltpu.SemaphoreType.DMA
    square = jax.ShapeDtypeStruct((width, width), jnp.float32)
    lower, solved = pl.pallas_call(
        functools.partial(kernel, nodes, levels),
        out_shape=(square, square),
        in_specs=[pl.BlockSpec(memory_space=pltpu.SMEM), vmem, vmem],
        out_specs=(vmem, vmem),
        scratch_shapes=[
            pltpu.VMEM((width, 2 * width), jnp.float32),
            pltpu.VMEM((width, 2 * width), jnp.float32),
            pltpu.VMEM((steps, width, width), jnp.float32),
            pltpu.VMEM((steps, width, width), jnp.float32),
            pltpu.VMEM((steps, width, 2 * width), jnp.bfloat16),
            pltpu.VMEM((steps, width, 2 * width), jnp.bfloat16),
            dma((steps,)), dma((steps,)), dma((steps, 2)), dma((steps, 2)),
        ] + [pltpu.VMEM((nodes, width, width), jnp.bfloat16)] * steps,
        compiler_params=pltpu.CompilerParams(collective_id=0, has_side_effects=True),
    )(targets, diag_blocks.reshape(width, width), panel_blocks.reshape(width, width))
    return lower[None], solved[None, None]


def solution(mesh):
    return jax.shard_map(
        shards,
        mesh=mesh,
        in_specs=(P("col", None, None), P("col", "grp", None, None), P()),
        out_specs=(P("col", None, None), P("col", "grp", None, None)),
        check_vma=False,
    )
```

```python
import functools

import jax
import jax.numpy as jnp
from jax import lax
from jax.experimental import pallas as pl
from jax.experimental.pallas import tpu as pltpu
from jax.sharding import PartitionSpec as P

MESH = pl.DeviceIdType.MESH
BLOCK = 16
HIGHEST = lax.Precision.HIGHEST


def across(value, width):
    return jnp.broadcast_to(value, (value.shape[0], width))


def factor_rows(work, width):
    total = 2 * width
    for first in range(0, width, BLOCK):
        rows = work[first:first + BLOCK, :]
        columns = [across(rows[:, first + j:first + j + 1], 128) for j in range(BLOCK)]
        index = lax.broadcasted_iota(jnp.int32, (BLOCK, 128), 0)
        done = []
        for j in range(BLOCK):
            pivot = columns[j][j:j + 1, :]
            inverse = lax.rsqrt(pivot)
            scaled = columns[j] * inverse
            below = jnp.where(index > j, scaled, 0.0)
            for k in range(j + 1, BLOCK):
                entry = scaled[k:k + 1, :]
                columns[k] = columns[k] - below * entry
            lead = [rows[j:j + 1, h:h + 128] * inverse for h in range(0, total, 128)]
            lead = jnp.concatenate(lead, 1)
            done.append(lead)
            if j + 1 < BLOCK:
                wide = jnp.concatenate([below] * (total // 128), 1)
                rows = rows - wide * lead
        upper = jnp.concatenate(done, 0)
        work[first:first + BLOCK, :] = upper
        if first + BLOCK < width:
            left = upper[:, :width]
            change = lax.dot_general(left, upper, (((0,), (0,)), ((), ())),
                                     precision=HIGHEST, preferred_element_type=jnp.float32)
            work[first + BLOCK:, :] = work[first + BLOCK:, :] - change[first + BLOCK:, :]


def kernel(nodes, levels, inner, targets, diag, panel, out_diag, out_panel, acc, work, depths, part,
           got_part, kids_out, kids_in, line_send, line_recv, plane_send, plane_recv, pair_send,
           pair_recv, *slots):
    width = diag.shape[-1]
    lines = nodes // inner
    me = lax.axis_index("col")
    core = lax.axis_index("grp")
    my_line = lax.div(me, inner)
    my_spot = lax.rem(me, inner)

    def along(offset):
        return lax.rem(my_line + offset, lines) * inner + my_spot

    def within(offset):
        return my_line * inner + lax.rem(my_spot + offset, inner)

    barrier = pltpu.get_barrier_semaphore()
    peers = [along(o) for o in range(1, lines)] + [within(o) for o in range(1, inner)]
    for peer in peers:
        pl.semaphore_signal(barrier, inc=1, device_id=(peer, core), device_id_type=MESH)
    pl.semaphore_signal(barrier, inc=1, device_id=(me, 1 - core), device_id_type=MESH)

    acc[:, :width] = diag[...]
    acc[:, width:] = panel[...].T

    def parent_of(node):
        return jnp.where(node < nodes, targets[jnp.minimum(node, nodes - 1), 0], nodes)

    def search(node, carry):
        current = targets[node, 0]
        kid = current == me
        grand = targets[node, 1] == me
        level = jnp.int32(0)
        for _ in range(levels - 1):
            level = level + (current < nodes).astype(jnp.int32)
            current = parent_of(current)
        depths[node] = level
        k0, k1, kc, g0, g1, g2, g3, gc = carry
        k0 = jnp.where(kid & (kc == 0), node, k0)
        k1 = jnp.where(kid & (kc == 1), node, k1)
        kc = kc + kid.astype(jnp.int32)
        g0 = jnp.where(grand & (gc == 0), node, g0)
        g1 = jnp.where(grand & (gc == 1), node, g1)
        g2 = jnp.where(grand & (gc == 2), node, g2)
        g3 = jnp.where(grand & (gc == 3), node, g3)
        gc = gc + grand.astype(jnp.int32)
        return k0, k1, kc, g0, g1, g2, g3, gc

    zero = jnp.int32(0)
    k0, k1, kc, g0, g1, g2, g3, gc = lax.fori_loop(0, nodes, search, (zero,) * 8)
    depth = depths[me]
    near_core = core == 0
    picks = [jnp.where(near_core, k0, g0), jnp.where(near_core, k1, g1), g2, g3]
    own_count = jnp.where(near_core, kc, gc)
    own_apart = jnp.where(near_core, 1, 2)

    def remote(src, dst, send_sem, recv_sem, peer):
        return pltpu.make_async_remote_copy(
            src_ref=src, dst_ref=dst, send_sem=send_sem, recv_sem=recv_sem,
            device_id=(peer, core), device_id_type=MESH)

    def send(step, slot_list, solved):
        if step == 0:
            pl.semaphore_wait(barrier, len(peers) + 1)
        level = levels - 1 - step
        planes = slot_list[0]
        column = slot_list[1] if len(slot_list) > 1 else planes.at[my_spot]
        column[my_line] = solved.astype(jnp.bfloat16)
        mine = column.at[my_line]
        for o in range(1, lines):
            remote(mine, mine, line_send.at[step], line_recv.at[step, o - 1], along(o)).start()

        def spread(ref):
            for o in range(1, inner):
                remote(ref, ref, plane_send.at[step], plane_recv.at[step], within(o)).start()

        def landed(o):
            from_line = column.at[lax.rem(my_line + lines - o, lines)]
            pltpu.make_async_copy(from_line, from_line, line_recv.at[step, o - 1]).wait()
            return from_line

        if len(slot_list) == 1:
            spread(mine)
            for o in range(1, lines):
                spread(landed(o))
        else:
            keep = planes.shape[1]
            chosen = [zero] * keep
            count = zero
            for q in range(lines):
                here = depths[q * inner + my_spot] == level
                chosen = [jnp.where(here & (count == j), q, chosen[j]) for j in range(keep)]
                count = count + here.astype(jnp.int32)
            for o in range(1, lines):
                landed(o)
            for j in range(keep):
                planes[my_spot, j] = column[chosen[j]]
            spread(planes.at[my_spot])

    def gather(step, slot_list):
        level = levels - 1 - step
        planes = slot_list[0]

        def pick(node, wanted):
            line = lax.div(node, inner)
            spot = lax.rem(node, inner)
            if len(slot_list) > 1:
                place = zero
                for q in range(lines):
                    here = (depths[q * inner + spot] == level) & (q < line)
                    place = place + here.astype(jnp.int32)
                place = jnp.minimum(place, planes.shape[1] - 1)
            else:
                place = line
            rows = planes[spot, place]
            return jnp.where(wanted, rows, jnp.zeros_like(rows))

        everyone = planes.at[pl.ds(0, inner - 1)]
        pltpu.make_async_copy(everyone, everyone, plane_recv.at[step]).wait()
        is_kid = depth + 1 == level
        kid_a = pick(k0, is_kid & (kc > 0))
        kid_b = pick(k1, is_kid & (kc > 1))
        kids_out[step, :, :width] = kid_a
        kids_out[step, :, width:] = kid_b
        rows_copy = pltpu.make_async_remote_copy(
            src_ref=kids_out.at[step], dst_ref=kids_in.at[step],
            send_sem=pair_send.at[step, 0], recv_sem=pair_recv.at[step, 0],
            device_id=(me, 1 - core), device_id_type=MESH)
        rows_copy.start()
        mine = depth + own_apart == level
        four = [pick(picks[j], mine & (own_count > j)) for j in range(4)]
        four = jnp.concatenate(four, 1)
        own = lax.dot_general(four, four, (((1,), (1,)), ((), ())),
                              preferred_element_type=jnp.float32)
        part[step] = own
        part_copy = pltpu.make_async_remote_copy(
            src_ref=part.at[step], dst_ref=got_part.at[step],
            send_sem=pair_send.at[step, 1], recv_sem=pair_recv.at[step, 1],
            device_id=(me, 1 - core), device_id_type=MESH)
        part_copy.start()
        rows_copy.wait()
        kids = jnp.concatenate([kid_a, kid_b], 1)
        cross = lax.dot_general(kids, kids_in[step], (((1,), (1,)), ((), ())),
                                preferred_element_type=jnp.float32)
        acc[:, width:] = acc[:, width:] - jnp.where(near_core, cross, 0.0)
        part_copy.wait()
        acc[:, :width] = acc[:, :width] - (own + got_part[step])
        pltpu.make_async_copy(everyone, everyone, plane_send.at[step]).wait()
        column = slot_list[1] if len(slot_list) > 1 else planes.at[0]
        others = column.at[pl.ds(0, lines - 1)]
        pltpu.make_async_copy(others, others, line_send.at[step]).wait()

    slots = list(slots)
    slot_lists = []
    for step in range(levels - 1):
        compact = slots[0].shape[1] < lines
        slot_lists.append([slots.pop(0) for _ in range(1 + compact)])

    def level_step(step, carry):
        level = levels - 1 - step
        work[...] = acc[...]
        factor_rows(work, width)
        solved = work[:, width:].T
        active = depth == level

        for turn in range(levels - 1):
            pl.when(step == turn)(functools.partial(send, turn, slot_lists[turn], solved))

        tri = lax.broadcasted_iota(jnp.int32, (width, width), 0)
        tri = tri >= lax.broadcasted_iota(jnp.int32, (width, width), 1)
        lower = jnp.where(tri, work[:, :width].T, 0.0)
        out_diag[...] = jnp.where(active, lower, out_diag[...])
        out_panel[...] = jnp.where(active, solved, out_panel[...])

        for turn in range(levels - 1):
            pl.when(step == turn)(functools.partial(gather, turn, slot_lists[turn]))

        return carry

    out_diag[...] = jnp.zeros_like(out_diag)
    out_panel[...] = jnp.zeros_like(out_panel)
    lax.fori_loop(0, levels, level_step, 0)


def shards(diag_blocks, panel_blocks, targets):
    width = diag_blocks.shape[1]
    nodes = targets.shape[0]
    levels = nodes.bit_length()
    steps = levels - 1
    inner = 1
    while inner * inner * 4 <= nodes:
        inner *= 2
    lines = nodes // inner
    slots = []
    for level in range(levels - 1, 0, -1):
        present = min(2**level, nodes - 2**level + 1)
        keep = min(lines, present)
        slots.append(pltpu.VMEM((inner, keep, width, width), jnp.bfloat16))
        if keep < lines:
            slots.append(pltpu.VMEM((lines, width, width), jnp.bfloat16))
    vmem = pl.BlockSpec(memory_space=pltpu.VMEM)
    dma = pltpu.SemaphoreType.DMA
    square = jax.ShapeDtypeStruct((width, width), jnp.float32)
    lower, solved = pl.pallas_call(
        functools.partial(kernel, nodes, levels, inner),
        out_shape=(square, square),
        in_specs=[pl.BlockSpec(memory_space=pltpu.SMEM), vmem, vmem],
        out_specs=(vmem, vmem),
        scratch_shapes=[
            pltpu.VMEM((width, 2 * width), jnp.float32),
            pltpu.VMEM((width, 2 * width), jnp.float32),
            pltpu.SMEM((nodes,), jnp.int32),
            pltpu.VMEM((steps, width, width), jnp.float32),
            pltpu.VMEM((steps, width, width), jnp.float32),
            pltpu.VMEM((steps, width, 2 * width), jnp.bfloat16),
            pltpu.VMEM((steps, width, 2 * width), jnp.bfloat16),
            dma((steps,)), dma((steps, lines - 1)), dma((steps,)), dma((steps,)),
            dma((steps, 2)), dma((steps, 2)),
        ] + slots,
        compiler_params=pltpu.CompilerParams(collective_id=0, has_side_effects=True),
    )(targets, diag_blocks.reshape(width, width), panel_blocks.reshape(width, width))
    return lower[None], solved[None, None]


def solution(mesh):
    return jax.shard_map(
        shards,
        mesh=mesh,
        in_specs=(P("col", None, None), P("col", "grp", None, None), P()),
        out_specs=(P("col", None, None), P("col", "grp", None, None)),
        check_vma=False,
    )
```

```python
import functools

import jax
import jax.numpy as jnp
from jax import lax
from jax.experimental import pallas as pl
from jax.experimental.pallas import tpu as pltpu
from jax.sharding import PartitionSpec as P

MESH = pl.DeviceIdType.MESH
BLOCK = 16
HALVES = 2
HIGHEST = lax.Precision.HIGHEST


def across(value, width):
    return jnp.broadcast_to(value, (value.shape[0], width))


def factor_rows(work, width, start, stop):
    total = 2 * width
    for first in range(start, stop, BLOCK):
        rows = work[first:first + BLOCK, :]
        columns = [across(rows[:, first + j:first + j + 1], 128) for j in range(BLOCK)]
        index = lax.broadcasted_iota(jnp.int32, (BLOCK, 128), 0)
        done = []
        for j in range(BLOCK):
            pivot = columns[j][j:j + 1, :]
            inverse = lax.rsqrt(pivot)
            scaled = columns[j] * inverse
            below = jnp.where(index > j, scaled, 0.0)
            for k in range(j + 1, BLOCK):
                entry = scaled[k:k + 1, :]
                columns[k] = columns[k] - below * entry
            lead = [rows[j:j + 1, h:h + 128] * inverse for h in range(0, total, 128)]
            lead = jnp.concatenate(lead, 1)
            done.append(lead)
            if j + 1 < BLOCK:
                wide = jnp.concatenate([below] * (total // 128), 1)
                rows = rows - wide * lead
        upper = jnp.concatenate(done, 0)
        work[first:first + BLOCK, :] = upper
        if first + BLOCK < width:
            left = upper[:, :width]
            change = lax.dot_general(left, upper, (((0,), (0,)), ((), ())),
                                     precision=HIGHEST, preferred_element_type=jnp.float32)
            work[first + BLOCK:, :] = work[first + BLOCK:, :] - change[first + BLOCK:, :]


def kernel(nodes, levels, inner, targets, diag, panel, out_diag, out_panel, acc, work, depths, part,
           got_part, kids_out, kids_in, line_send, line_recv, plane_send, plane_recv, pair_send,
           pair_recv, *slots):
    width = diag.shape[-1]
    depth_rows = width // HALVES
    lines = nodes // inner
    me = lax.axis_index("col")
    core = lax.axis_index("grp")
    my_line = lax.div(me, inner)
    my_spot = lax.rem(me, inner)

    def along(offset):
        return lax.rem(my_line + offset, lines) * inner + my_spot

    def within(offset):
        return my_line * inner + lax.rem(my_spot + offset, inner)

    barrier = pltpu.get_barrier_semaphore()
    peers = [along(o) for o in range(1, lines)] + [within(o) for o in range(1, inner)]
    for peer in peers:
        pl.semaphore_signal(barrier, inc=1, device_id=(peer, core), device_id_type=MESH)
    pl.semaphore_signal(barrier, inc=1, device_id=(me, 1 - core), device_id_type=MESH)

    acc[:, :width] = diag[...]
    acc[:, width:] = panel[...].T

    def parent_of(node):
        return jnp.where(node < nodes, targets[jnp.minimum(node, nodes - 1), 0], nodes)

    def search(node, carry):
        current = targets[node, 0]
        kid = current == me
        grand = targets[node, 1] == me
        level = jnp.int32(0)
        for _ in range(levels - 1):
            level = level + (current < nodes).astype(jnp.int32)
            current = parent_of(current)
        depths[node] = level
        k0, k1, kc, g0, g1, g2, g3, gc = carry
        k0 = jnp.where(kid & (kc == 0), node, k0)
        k1 = jnp.where(kid & (kc == 1), node, k1)
        kc = kc + kid.astype(jnp.int32)
        g0 = jnp.where(grand & (gc == 0), node, g0)
        g1 = jnp.where(grand & (gc == 1), node, g1)
        g2 = jnp.where(grand & (gc == 2), node, g2)
        g3 = jnp.where(grand & (gc == 3), node, g3)
        gc = gc + grand.astype(jnp.int32)
        return k0, k1, kc, g0, g1, g2, g3, gc

    zero = jnp.int32(0)
    k0, k1, kc, g0, g1, g2, g3, gc = lax.fori_loop(0, nodes, search, (zero,) * 8)
    depth = depths[me]
    near_core = core == 0
    picks = [jnp.where(near_core, k0, g0), jnp.where(near_core, k1, g1), g2, g3]
    own_count = jnp.where(near_core, kc, gc)
    own_apart = jnp.where(near_core, 1, 2)

    def remote(src, dst, send_sem, recv_sem, peer):
        return pltpu.make_async_remote_copy(
            src_ref=src, dst_ref=dst, send_sem=send_sem, recv_sem=recv_sem,
            device_id=(peer, core), device_id_type=MESH)

    def column_of(slot_list):
        return slot_list[1] if len(slot_list) > 1 else slot_list[0].at[my_spot]

    def rows_of(half):
        return pl.ds(half * depth_rows, depth_rows)

    def spread(step, half, ref):
        for o in range(1, inner):
            remote(ref, ref, plane_send.at[step], plane_recv.at[step], within(o)).start()

    def send(step, slot_list, half):
        if step == 0 and half == 0:
            pl.semaphore_wait(barrier, len(peers) + 1)
        column = column_of(slot_list)
        mine = column.at[my_line, rows_of(half)]
        mine[...] = work[rows_of(half), width:].astype(jnp.bfloat16)
        for o in range(1, lines):
            remote(mine, mine, line_send.at[step], line_recv.at[step, half, o - 1],
                   along(o)).start()
        if len(slot_list) == 1:
            spread(step, half, mine)

    def relay(step, slot_list):
        level = levels - 1 - step
        planes = slot_list[0]
        column = column_of(slot_list)

        def landed(half, o):
            from_line = column.at[lax.rem(my_line + lines - o, lines), rows_of(half)]
            pltpu.make_async_copy(from_line, from_line, line_recv.at[step, half, o - 1]).wait()
            return from_line

        if len(slot_list) == 1:
            for half in range(HALVES):
                for o in range(1, lines):
                    spread(step, half, landed(half, o))
        else:
            keep = planes.shape[1]
            chosen = [zero] * keep
            count = zero
            for q in range(lines):
                here = depths[q * inner + my_spot] == level
                chosen = [jnp.where(here & (count == j), q, chosen[j]) for j in range(keep)]
                count = count + here.astype(jnp.int32)
            for half in range(HALVES):
                for o in range(1, lines):
                    landed(half, o)
            for j in range(keep):
                planes[my_spot, j] = column[chosen[j]]
            spread(step, 0, planes.at[my_spot])

    def gather(step, slot_list):
        level = levels - 1 - step
        planes = slot_list[0]

        def pick(node, wanted):
            line = lax.div(node, inner)
            spot = lax.rem(node, inner)
            if len(slot_list) > 1:
                place = zero
                for q in range(lines):
                    here = (depths[q * inner + spot] == level) & (q < line)
                    place = place + here.astype(jnp.int32)
                place = jnp.minimum(place, planes.shape[1] - 1)
            else:
                place = line
            rows = planes[spot, place]
            return jnp.where(wanted, rows, jnp.zeros_like(rows))

        everyone = planes.at[pl.ds(0, inner - 1)]
        pltpu.make_async_copy(everyone, everyone, plane_recv.at[step]).wait()
        is_kid = depth + 1 == level
        kid_a = pick(k0, is_kid & (kc > 0))
        kid_b = pick(k1, is_kid & (kc > 1))
        kids_out[step, :width] = kid_a
        kids_out[step, width:] = kid_b
        rows_copy = pltpu.make_async_remote_copy(
            src_ref=kids_out.at[step], dst_ref=kids_in.at[step],
            send_sem=pair_send.at[step, 0], recv_sem=pair_recv.at[step, 0],
            device_id=(me, 1 - core), device_id_type=MESH)
        pl.when(core == 1)(rows_copy.start)
        mine = depth + own_apart == level
        four = [pick(picks[j], mine & (own_count > j)) for j in range(4)]
        four = jnp.concatenate(four, 0)
        own = lax.dot_general(four, four, (((0,), (0,)), ((), ())),
                              preferred_element_type=jnp.float32)
        part[step] = own
        part_copy = pltpu.make_async_remote_copy(
            src_ref=part.at[step], dst_ref=got_part.at[step],
            send_sem=pair_send.at[step, 1], recv_sem=pair_recv.at[step, 1],
            device_id=(me, 1 - core), device_id_type=MESH)
        part_copy.start()

        @pl.when(core == 0)
        def _():
            rows_copy.wait_recv()
            kids = jnp.concatenate([kid_a, kid_b], 0)
            cross = lax.dot_general(kids, kids_in[step], (((0,), (0,)), ((), ())),
                                    preferred_element_type=jnp.float32)
            acc[:, width:] = acc[:, width:] - cross

        part_copy.wait_recv()
        acc[:, :width] = acc[:, :width] - (own + got_part[step])

    def settle(step, slot_list):
        planes = slot_list[0]
        everyone = planes.at[pl.ds(0, inner - 1)]
        pltpu.make_async_copy(everyone, everyone, plane_send.at[step]).wait()
        others = column_of(slot_list).at[pl.ds(0, lines - 1)]
        pltpu.make_async_copy(others, others, line_send.at[step]).wait()
        sent = part.at[step]
        pltpu.make_async_copy(sent, sent, pair_send.at[step, 1]).wait()

        @pl.when(core == 1)
        def _():
            kids = kids_out.at[step]
            pltpu.make_async_copy(kids, kids, pair_send.at[step, 0]).wait()

    slots = list(slots)
    slot_lists = []
    for step in range(levels - 1):
        compact = slots[0].shape[1] < lines
        slot_lists.append([slots.pop(0) for _ in range(1 + compact)])

    def level_step(step, carry):
        level = levels - 1 - step
        work[...] = acc[...]
        active = depth == level
        for half in range(HALVES):
            factor_rows(work, width, half * depth_rows, (half + 1) * depth_rows)
            for turn in range(levels - 1):
                pl.when(step == turn)(functools.partial(send, turn, slot_lists[turn], half))

        for turn in range(levels - 1):
            pl.when(step == turn)(functools.partial(relay, turn, slot_lists[turn]))

        tri = lax.broadcasted_iota(jnp.int32, (width, width), 0)
        tri = tri >= lax.broadcasted_iota(jnp.int32, (width, width), 1)
        lower = jnp.where(tri, work[:, :width].T, 0.0)
        out_diag[...] = jnp.where(active, lower, out_diag[...])
        out_panel[...] = jnp.where(active, work[:, width:].T, out_panel[...])

        for turn in range(levels - 1):
            pl.when(step == turn)(functools.partial(gather, turn, slot_lists[turn]))

        return carry

    out_diag[...] = jnp.zeros_like(out_diag)
    out_panel[...] = jnp.zeros_like(out_panel)
    lax.fori_loop(0, levels, level_step, 0)
    for turn in range(levels - 1):
        settle(turn, slot_lists[turn])


def shards(diag_blocks, panel_blocks, targets):
    width = diag_blocks.shape[1]
    nodes = targets.shape[0]
    levels = nodes.bit_length()
    steps = levels - 1
    inner = 1
    while inner * inner * 4 <= nodes:
        inner *= 2
    lines = nodes // inner
    slots = []
    for level in range(levels - 1, 0, -1):
        present = min(2**level, nodes - 2**level + 1)
        keep = min(lines, present)
        slots.append(pltpu.VMEM((inner, keep, width, width), jnp.bfloat16))
        if keep < lines:
            slots.append(pltpu.VMEM((lines, width, width), jnp.bfloat16))
    vmem = pl.BlockSpec(memory_space=pltpu.VMEM)
    dma = pltpu.SemaphoreType.DMA
    square = jax.ShapeDtypeStruct((width, width), jnp.float32)
    lower, solved = pl.pallas_call(
        functools.partial(kernel, nodes, levels, inner),
        out_shape=(square, square),
        in_specs=[pl.BlockSpec(memory_space=pltpu.SMEM), vmem, vmem],
        out_specs=(vmem, vmem),
        scratch_shapes=[
            pltpu.VMEM((width, 2 * width), jnp.float32),
            pltpu.VMEM((width, 2 * width), jnp.float32),
            pltpu.SMEM((nodes,), jnp.int32),
            pltpu.VMEM((steps, width, width), jnp.float32),
            pltpu.VMEM((steps, width, width), jnp.float32),
            pltpu.VMEM((steps, 2 * width, width), jnp.bfloat16),
            pltpu.VMEM((steps, 2 * width, width), jnp.bfloat16),
            dma((steps,)), dma((steps, HALVES, lines - 1)), dma((steps,)), dma((steps,)),
            dma((steps, 2)), dma((steps, 2)),
        ] + slots,
        compiler_params=pltpu.CompilerParams(collective_id=0, has_side_effects=True),
    )(targets, diag_blocks.reshape(width, width), panel_blocks.reshape(width, width))
    return lower[None], solved[None, None]


def solution(mesh):
    return jax.shard_map(
        shards,
        mesh=mesh,
        in_specs=(P("col", None, None), P("col", "grp", None, None), P()),
        out_specs=(P("col", None, None), P("col", "grp", None, None)),
        check_vma=False,
    )
```

```python
import functools

import jax
import jax.numpy as jnp
from jax import lax
from jax.experimental import pallas as pl
from jax.experimental.pallas import tpu as pltpu
from jax.sharding import PartitionSpec as P

MESH = pl.DeviceIdType.MESH
BLOCK = 16
HALVES = 2
HIGHEST = lax.Precision.HIGHEST


def across(value, width):
    return jnp.broadcast_to(value, (value.shape[0], width))


def factor_rows(work, width, start, stop):
    total = 2 * width
    for first in range(start, stop, BLOCK):
        rows = work[first:first + BLOCK, :]
        columns = [across(rows[:, first + j:first + j + 1], 128) for j in range(BLOCK)]
        index = lax.broadcasted_iota(jnp.int32, (BLOCK, 128), 0)
        done = []
        for j in range(BLOCK):
            pivot = columns[j][j:j + 1, :]
            inverse = lax.rsqrt(pivot)
            scaled = columns[j] * inverse
            below = jnp.where(index > j, scaled, 0.0)
            for k in range(j + 1, BLOCK):
                entry = scaled[k:k + 1, :]
                columns[k] = columns[k] - below * entry
            lead = [rows[j:j + 1, h:h + 128] * inverse for h in range(0, total, 128)]
            lead = jnp.concatenate(lead, 1)
            done.append(lead)
            if j + 1 < BLOCK:
                wide = jnp.concatenate([below] * (total // 128), 1)
                rows = rows - wide * lead
        upper = jnp.concatenate(done, 0)
        work[first:first + BLOCK, :] = upper
        if first + BLOCK < width:
            left = upper[:, :width]
            change = lax.dot_general(left, upper, (((0,), (0,)), ((), ())),
                                     precision=HIGHEST, preferred_element_type=jnp.float32)
            work[first + BLOCK:, :] = work[first + BLOCK:, :] - change[first + BLOCK:, :]


def kernel(nodes, levels, inner, targets, diag, panel, out_diag, out_panel, acc, work, depths, part,
           got_part, kids_out, kids_in, line_send, line_recv, plane_send, plane_recv, pair_send,
           pair_recv, *slots):
    width = diag.shape[-1]
    depth_rows = width // HALVES
    lines = nodes // inner
    me = lax.axis_index("col")
    core = lax.axis_index("grp")
    my_line = lax.div(me, inner)
    my_spot = lax.rem(me, inner)

    def along(offset):
        return lax.rem(my_line + offset, lines) * inner + my_spot

    def within(offset):
        return my_line * inner + lax.rem(my_spot + offset, inner)

    barrier = pltpu.get_barrier_semaphore()
    peers = [along(o) for o in range(1, lines)] + [within(o) for o in range(1, inner)]
    for peer in peers:
        pl.semaphore_signal(barrier, inc=1, device_id=(peer, core), device_id_type=MESH)
    pl.semaphore_signal(barrier, inc=1, device_id=(me, 1 - core), device_id_type=MESH)

    acc[:, :width] = diag[...]
    acc[:, width:] = panel[...].T

    def parent_of(node):
        return jnp.where(node < nodes, targets[0, jnp.minimum(node, nodes - 1)], nodes)

    def search(node, carry):
        current = targets[0, node]
        kid = current == me
        grand = targets[1, node] == me
        level = jnp.int32(0)
        for _ in range(levels - 1):
            level = level + (current < nodes).astype(jnp.int32)
            current = parent_of(current)
        depths[node] = level
        k0, k1, kc, g0, g1, g2, g3, gc = carry
        k0 = jnp.where(kid & (kc == 0), node, k0)
        k1 = jnp.where(kid & (kc == 1), node, k1)
        kc = kc + kid.astype(jnp.int32)
        g0 = jnp.where(grand & (gc == 0), node, g0)
        g1 = jnp.where(grand & (gc == 1), node, g1)
        g2 = jnp.where(grand & (gc == 2), node, g2)
        g3 = jnp.where(grand & (gc == 3), node, g3)
        gc = gc + grand.astype(jnp.int32)
        return k0, k1, kc, g0, g1, g2, g3, gc

    zero = jnp.int32(0)
    k0, k1, kc, g0, g1, g2, g3, gc = lax.fori_loop(0, nodes, search, (zero,) * 8)
    depth = depths[me]
    near_core = core == 0
    picks = [jnp.where(near_core, k0, g0), jnp.where(near_core, k1, g1), g2, g3]
    own_count = jnp.where(near_core, kc, gc)
    own_apart = jnp.where(near_core, 1, 2)

    def remote(src, dst, send_sem, recv_sem, peer):
        return pltpu.make_async_remote_copy(
            src_ref=src, dst_ref=dst, send_sem=send_sem, recv_sem=recv_sem,
            device_id=(peer, core), device_id_type=MESH)

    def column_of(slot_list):
        return slot_list[1] if len(slot_list) > 1 else slot_list[0].at[my_spot]

    def rows_of(half):
        return pl.ds(half * depth_rows, depth_rows)

    def spread(step, half, ref):
        for o in range(1, inner):
            remote(ref, ref, plane_send.at[step], plane_recv.at[step], within(o)).start()

    def send(step, slot_list, half):
        if step == 0 and half == 0:
            pl.semaphore_wait(barrier, len(peers) + 1)
        column = column_of(slot_list)
        mine = column.at[my_line, rows_of(half)]
        mine[...] = work[rows_of(half), width:].astype(jnp.bfloat16)
        for o in range(1, lines):
            remote(mine, mine, line_send.at[step], line_recv.at[step, half, o - 1],
                   along(o)).start()
        if len(slot_list) == 1:
            spread(step, half, mine)

    def relay(step, slot_list):
        level = levels - 1 - step
        planes = slot_list[0]
        column = column_of(slot_list)

        def landed(half, o):
            from_line = column.at[lax.rem(my_line + lines - o, lines), rows_of(half)]
            pltpu.make_async_copy(from_line, from_line, line_recv.at[step, half, o - 1]).wait()
            return from_line

        if len(slot_list) == 1:
            for half in range(HALVES):
                for o in range(1, lines):
                    spread(step, half, landed(half, o))
        else:
            keep = planes.shape[1]
            chosen = [zero] * keep
            count = zero
            for q in range(lines):
                here = depths[q * inner + my_spot] == level
                chosen = [jnp.where(here & (count == j), q, chosen[j]) for j in range(keep)]
                count = count + here.astype(jnp.int32)
            for half in range(HALVES):
                for o in range(1, lines):
                    landed(half, o)
            for j in range(keep):
                planes[my_spot, j] = column[chosen[j]]
            spread(step, 0, planes.at[my_spot])

    def gather(step, slot_list):
        level = levels - 1 - step
        planes = slot_list[0]

        def pick(node, wanted):
            line = lax.div(node, inner)
            spot = lax.rem(node, inner)
            if len(slot_list) > 1:
                place = zero
                for q in range(lines):
                    here = (depths[q * inner + spot] == level) & (q < line)
                    place = place + here.astype(jnp.int32)
                place = jnp.minimum(place, planes.shape[1] - 1)
            else:
                place = line
            rows = planes[spot, place]
            return jnp.where(wanted, rows, jnp.zeros_like(rows))

        everyone = planes.at[pl.ds(0, inner - 1)]
        pltpu.make_async_copy(everyone, everyone, plane_recv.at[step]).wait()
        is_kid = depth + 1 == level
        kid_a = pick(k0, is_kid & (kc > 0))
        kid_b = pick(k1, is_kid & (kc > 1))
        kids_out[step, :width] = kid_a
        kids_out[step, width:] = kid_b
        rows_copy = pltpu.make_async_remote_copy(
            src_ref=kids_out.at[step], dst_ref=kids_in.at[step],
            send_sem=pair_send.at[step, 0], recv_sem=pair_recv.at[step, 0],
            device_id=(me, 1 - core), device_id_type=MESH)
        pl.when(core == 1)(rows_copy.start)
        mine = depth + own_apart == level
        four = [pick(picks[j], mine & (own_count > j)) for j in range(4)]
        four = jnp.concatenate(four, 0)
        own = lax.dot_general(four, four, (((0,), (0,)), ((), ())),
                              preferred_element_type=jnp.float32)
        part[step] = own
        part_copy = pltpu.make_async_remote_copy(
            src_ref=part.at[step], dst_ref=got_part.at[step],
            send_sem=pair_send.at[step, 1], recv_sem=pair_recv.at[step, 1],
            device_id=(me, 1 - core), device_id_type=MESH)
        part_copy.start()

        @pl.when(core == 0)
        def _():
            rows_copy.wait_recv()
            kids = jnp.concatenate([kid_a, kid_b], 0)
            cross = lax.dot_general(kids, kids_in[step], (((0,), (0,)), ((), ())),
                                    preferred_element_type=jnp.float32)
            acc[:, width:] = acc[:, width:] - cross

        part_copy.wait_recv()
        acc[:, :width] = acc[:, :width] - (own + got_part[step])

    def settle(step, slot_list):
        planes = slot_list[0]
        everyone = planes.at[pl.ds(0, inner - 1)]
        pltpu.make_async_copy(everyone, everyone, plane_send.at[step]).wait()
        others = column_of(slot_list).at[pl.ds(0, lines - 1)]
        pltpu.make_async_copy(others, others, line_send.at[step]).wait()
        sent = part.at[step]
        pltpu.make_async_copy(sent, sent, pair_send.at[step, 1]).wait()

        @pl.when(core == 1)
        def _():
            kids = kids_out.at[step]
            pltpu.make_async_copy(kids, kids, pair_send.at[step, 0]).wait()

    slots = list(slots)
    slot_lists = []
    for step in range(levels - 1):
        compact = slots[0].shape[1] < lines
        slot_lists.append([slots.pop(0) for _ in range(1 + compact)])

    def level_step(step, carry):
        level = levels - 1 - step
        work[...] = acc[...]
        active = depth == level
        for half in range(HALVES):
            factor_rows(work, width, half * depth_rows, (half + 1) * depth_rows)
            for turn in range(levels - 1):
                pl.when(step == turn)(functools.partial(send, turn, slot_lists[turn], half))

        for turn in range(levels - 1):
            pl.when(step == turn)(functools.partial(relay, turn, slot_lists[turn]))

        tri = lax.broadcasted_iota(jnp.int32, (width, width), 0)
        tri = tri >= lax.broadcasted_iota(jnp.int32, (width, width), 1)
        lower = jnp.where(tri, work[:, :width].T, 0.0)
        out_diag[...] = jnp.where(active, lower, out_diag[...])
        out_panel[...] = jnp.where(active, work[:, width:].T, out_panel[...])

        for turn in range(levels - 1):
            pl.when(step == turn)(functools.partial(gather, turn, slot_lists[turn]))

        return carry

    out_diag[...] = jnp.zeros_like(out_diag)
    out_panel[...] = jnp.zeros_like(out_panel)
    lax.fori_loop(0, levels, level_step, 0)
    for turn in range(levels - 1):
        settle(turn, slot_lists[turn])


def shards(diag_blocks, panel_blocks, targets):
    width = diag_blocks.shape[1]
    nodes = targets.shape[0]
    levels = nodes.bit_length()
    steps = levels - 1
    inner = 1
    while inner * inner * 4 <= nodes:
        inner *= 2
    lines = nodes // inner
    slots = []
    for level in range(levels - 1, 0, -1):
        present = min(2**level, nodes - 2**level + 1)
        keep = min(lines, present)
        slots.append(pltpu.VMEM((inner, keep, width, width), jnp.bfloat16))
        if keep < lines:
            slots.append(pltpu.VMEM((lines, width, width), jnp.bfloat16))
    vmem = pl.BlockSpec(memory_space=pltpu.VMEM)
    dma = pltpu.SemaphoreType.DMA
    square = pltpu.VMEM((width, width), jnp.float32)
    lower, solved = pl.pallas_call(
        functools.partial(kernel, nodes, levels, inner),
        out_shape=(square, square),
        in_specs=[pl.BlockSpec(memory_space=pltpu.SMEM), vmem, vmem],
        out_specs=(vmem, vmem),
        scratch_shapes=[
            pltpu.VMEM((width, 2 * width), jnp.float32),
            pltpu.VMEM((width, 2 * width), jnp.float32),
            pltpu.SMEM((nodes,), jnp.int32),
            pltpu.VMEM((steps, width, width), jnp.float32),
            pltpu.VMEM((steps, width, width), jnp.float32),
            pltpu.VMEM((steps, 2 * width, width), jnp.bfloat16),
            pltpu.VMEM((steps, 2 * width, width), jnp.bfloat16),
            dma((steps,)), dma((steps, HALVES, lines - 1)), dma((steps,)), dma((steps,)),
            dma((steps, 2)), dma((steps, 2)),
        ] + slots,
        compiler_params=pltpu.CompilerParams(collective_id=0, has_side_effects=True),
    )(targets.T, diag_blocks.reshape(width, width), panel_blocks.reshape(width, width))
    return lower[None], solved[None, None]


def solution(mesh):
    return jax.shard_map(
        shards,
        mesh=mesh,
        in_specs=(P("col", None, None), P("col", "grp", None, None), P()),
        out_specs=(P("col", None, None), P("col", "grp", None, None)),
        check_vma=False,
    )
```

```python
import functools

import jax
import jax.numpy as jnp
from jax import lax
from jax.experimental import pallas as pl
from jax.experimental.pallas import tpu as pltpu
from jax.sharding import PartitionSpec as P

MESH = pl.DeviceIdType.MESH
BLOCK = 32
HALVES = 2
HIGHEST = lax.Precision.HIGHEST


def across(value, width):
    return jnp.broadcast_to(value, (value.shape[0], width))


def factor_rows(work, width, start, stop):
    total = 2 * width
    for first in range(start, stop, BLOCK):
        rows = work[first:first + BLOCK, :]
        columns = [across(rows[:, first + j:first + j + 1], 128) for j in range(BLOCK)]
        index = lax.broadcasted_iota(jnp.int32, (BLOCK, 128), 0)
        done = []
        for j in range(BLOCK):
            pivot = columns[j][j:j + 1, :]
            inverse = lax.rsqrt(pivot)
            scaled = columns[j] * inverse
            below = jnp.where(index > j, scaled, 0.0)
            for k in range(j + 1, BLOCK):
                entry = scaled[k:k + 1, :]
                columns[k] = columns[k] - below * entry
            lead = [rows[j:j + 1, h:h + 128] * inverse for h in range(0, total, 128)]
            lead = jnp.concatenate(lead, 1)
            done.append(lead)
            if j + 1 < BLOCK:
                wide = jnp.concatenate([below] * (total // 128), 1)
                rows = rows - wide * lead
        upper = jnp.concatenate(done, 0)
        work[first:first + BLOCK, :] = upper
        if first + BLOCK < width:
            high = upper.astype(jnp.bfloat16)
            rest = upper - high.astype(jnp.float32)
            middle = rest.astype(jnp.bfloat16)
            low = (rest - middle.astype(jnp.float32)).astype(jnp.bfloat16)
            left = [term[:, :width] for term in (high, high, high, middle, middle, low)]
            left = jnp.concatenate(left, 0)
            right = jnp.concatenate([high, middle, low, high, middle, high], 0)
            change = lax.dot_general(left, right, (((0,), (0,)), ((), ())),
                                     preferred_element_type=jnp.float32)
            work[first + BLOCK:, :] = work[first + BLOCK:, :] - change[first + BLOCK:, :]


def kernel(nodes, levels, inner, targets, diag, panel, out_diag, out_panel, acc, work, depths, part,
           got_part, kids_out, kids_in, line_send, line_recv, plane_send, plane_recv, pair_send,
           pair_recv, *slots):
    width = diag.shape[-1]
    depth_rows = width // HALVES
    lines = nodes // inner
    me = lax.axis_index("col")
    core = lax.axis_index("grp")
    my_line = lax.div(me, inner)
    my_spot = lax.rem(me, inner)

    def along(offset):
        return lax.rem(my_line + offset, lines) * inner + my_spot

    def within(offset):
        return my_line * inner + lax.rem(my_spot + offset, inner)

    barrier = pltpu.get_barrier_semaphore()
    peers = [along(o) for o in range(1, lines)] + [within(o) for o in range(1, inner)]
    for peer in peers:
        pl.semaphore_signal(barrier, inc=1, device_id=(peer, core), device_id_type=MESH)
    pl.semaphore_signal(barrier, inc=1, device_id=(me, 1 - core), device_id_type=MESH)

    acc[:, :width] = diag[...]
    acc[:, width:] = panel[...].T

    def parent_of(node):
        return jnp.where(node < nodes, targets[0, jnp.minimum(node, nodes - 1)], nodes)

    def search(node, carry):
        current = targets[0, node]
        kid = current == me
        grand = targets[1, node] == me
        level = jnp.int32(0)
        for _ in range(levels - 1):
            level = level + (current < nodes).astype(jnp.int32)
            current = parent_of(current)
        depths[node] = level
        k0, k1, kc, g0, g1, g2, g3, gc = carry
        k0 = jnp.where(kid & (kc == 0), node, k0)
        k1 = jnp.where(kid & (kc == 1), node, k1)
        kc = kc + kid.astype(jnp.int32)
        g0 = jnp.where(grand & (gc == 0), node, g0)
        g1 = jnp.where(grand & (gc == 1), node, g1)
        g2 = jnp.where(grand & (gc == 2), node, g2)
        g3 = jnp.where(grand & (gc == 3), node, g3)
        gc = gc + grand.astype(jnp.int32)
        return k0, k1, kc, g0, g1, g2, g3, gc

    zero = jnp.int32(0)
    k0, k1, kc, g0, g1, g2, g3, gc = lax.fori_loop(0, nodes, search, (zero,) * 8)
    depth = depths[me]
    near_core = core == 0
    picks = [jnp.where(near_core, k0, g0), jnp.where(near_core, k1, g1), g2, g3]
    own_count = jnp.where(near_core, kc, gc)
    own_apart = jnp.where(near_core, 1, 2)

    def remote(src, dst, send_sem, recv_sem, peer):
        return pltpu.make_async_remote_copy(
            src_ref=src, dst_ref=dst, send_sem=send_sem, recv_sem=recv_sem,
            device_id=(peer, core), device_id_type=MESH)

    def column_of(slot_list):
        return slot_list[1] if len(slot_list) > 1 else slot_list[0].at[my_spot]

    def rows_of(half):
        return pl.ds(half * depth_rows, depth_rows)

    def spread(step, half, ref):
        for o in range(1, inner):
            remote(ref, ref, plane_send.at[step], plane_recv.at[step], within(o)).start()

    def send(step, slot_list, half):
        if step == 0 and half == 0:
            pl.semaphore_wait(barrier, len(peers) + 1)
        column = column_of(slot_list)
        mine = column.at[my_line, rows_of(half)]
        mine[...] = work[rows_of(half), width:].astype(jnp.bfloat16)
        for o in range(1, lines):
            remote(mine, mine, line_send.at[step], line_recv.at[step, half, o - 1],
                   along(o)).start()
        if len(slot_list) == 1:
            spread(step, half, mine)

    def relay(step, slot_list):
        level = levels - 1 - step
        planes = slot_list[0]
        column = column_of(slot_list)

        def landed(half, o):
            from_line = column.at[lax.rem(my_line + lines - o, lines), rows_of(half)]
            pltpu.make_async_copy(from_line, from_line, line_recv.at[step, half, o - 1]).wait()
            return from_line

        if len(slot_list) == 1:
            for half in range(HALVES):
                for o in range(1, lines):
                    spread(step, half, landed(half, o))
        else:
            keep = planes.shape[1]
            chosen = [zero] * keep
            count = zero
            for q in range(lines):
                here = depths[q * inner + my_spot] == level
                chosen = [jnp.where(here & (count == j), q, chosen[j]) for j in range(keep)]
                count = count + here.astype(jnp.int32)
            for half in range(HALVES):
                for o in range(1, lines):
                    landed(half, o)
            for j in range(keep):
                planes[my_spot, j] = column[chosen[j]]
            spread(step, 0, planes.at[my_spot])

    def gather(step, slot_list):
        level = levels - 1 - step
        planes = slot_list[0]

        def pick(node, wanted):
            line = lax.div(node, inner)
            spot = lax.rem(node, inner)
            if len(slot_list) > 1:
                place = zero
                for q in range(lines):
                    here = (depths[q * inner + spot] == level) & (q < line)
                    place = place + here.astype(jnp.int32)
                place = jnp.minimum(place, planes.shape[1] - 1)
            else:
                place = line
            rows = planes[spot, place]
            return jnp.where(wanted, rows, jnp.zeros_like(rows))

        everyone = planes.at[pl.ds(0, inner - 1)]
        pltpu.make_async_copy(everyone, everyone, plane_recv.at[step]).wait()
        is_kid = depth + 1 == level
        kid_a = pick(k0, is_kid & (kc > 0))
        kid_b = pick(k1, is_kid & (kc > 1))
        kids_out[step, :width] = kid_a
        kids_out[step, width:] = kid_b
        rows_copy = pltpu.make_async_remote_copy(
            src_ref=kids_out.at[step], dst_ref=kids_in.at[step],
            send_sem=pair_send.at[step, 0], recv_sem=pair_recv.at[step, 0],
            device_id=(me, 1 - core), device_id_type=MESH)
        pl.when(core == 1)(rows_copy.start)
        mine = depth + own_apart == level
        four = [pick(picks[j], mine & (own_count > j)) for j in range(4)]
        four = jnp.concatenate(four, 0)
        own = lax.dot_general(four, four, (((0,), (0,)), ((), ())),
                              preferred_element_type=jnp.float32)
        part[step] = own
        part_copy = pltpu.make_async_remote_copy(
            src_ref=part.at[step], dst_ref=got_part.at[step],
            send_sem=pair_send.at[step, 1], recv_sem=pair_recv.at[step, 1],
            device_id=(me, 1 - core), device_id_type=MESH)
        part_copy.start()

        @pl.when(core == 0)
        def _():
            rows_copy.wait_recv()
            kids = jnp.concatenate([kid_a, kid_b], 0)
            cross = lax.dot_general(kids, kids_in[step], (((0,), (0,)), ((), ())),
                                    preferred_element_type=jnp.float32)
            acc[:, width:] = acc[:, width:] - cross

        part_copy.wait_recv()
        acc[:, :width] = acc[:, :width] - (own + got_part[step])

    def settle(step, slot_list):
        planes = slot_list[0]
        everyone = planes.at[pl.ds(0, inner - 1)]
        pltpu.make_async_copy(everyone, everyone, plane_send.at[step]).wait()
        others = column_of(slot_list).at[pl.ds(0, lines - 1)]
        pltpu.make_async_copy(others, others, line_send.at[step]).wait()
        sent = part.at[step]
        pltpu.make_async_copy(sent, sent, pair_send.at[step, 1]).wait()

        @pl.when(core == 1)
        def _():
            kids = kids_out.at[step]
            pltpu.make_async_copy(kids, kids, pair_send.at[step, 0]).wait()

    slots = list(slots)
    slot_lists = []
    for step in range(levels - 1):
        compact = slots[0].shape[1] < lines
        slot_lists.append([slots.pop(0) for _ in range(1 + compact)])

    def level_step(step, carry):
        level = levels - 1 - step
        work[...] = acc[...]
        active = depth == level
        for half in range(HALVES):
            factor_rows(work, width, half * depth_rows, (half + 1) * depth_rows)
            for turn in range(levels - 1):
                pl.when(step == turn)(functools.partial(send, turn, slot_lists[turn], half))

        for turn in range(levels - 1):
            pl.when(step == turn)(functools.partial(relay, turn, slot_lists[turn]))

        tri = lax.broadcasted_iota(jnp.int32, (width, width), 0)
        tri = tri >= lax.broadcasted_iota(jnp.int32, (width, width), 1)
        lower = jnp.where(tri, work[:, :width].T, 0.0)
        out_diag[...] = jnp.where(active, lower, out_diag[...])
        out_panel[...] = jnp.where(active, work[:, width:].T, out_panel[...])

        for turn in range(levels - 1):
            pl.when(step == turn)(functools.partial(gather, turn, slot_lists[turn]))

        return carry

    out_diag[...] = jnp.zeros_like(out_diag)
    out_panel[...] = jnp.zeros_like(out_panel)
    lax.fori_loop(0, levels, level_step, 0)
    for turn in range(levels - 1):
        settle(turn, slot_lists[turn])


def shards(diag_blocks, panel_blocks, targets):
    width = diag_blocks.shape[1]
    nodes = targets.shape[0]
    levels = nodes.bit_length()
    steps = levels - 1
    inner = 1
    while inner * inner * 4 <= nodes:
        inner *= 2
    lines = nodes // inner
    slots = []
    for level in range(levels - 1, 0, -1):
        present = min(2**level, nodes - 2**level + 1)
        keep = min(lines, present)
        slots.append(pltpu.VMEM((inner, keep, width, width), jnp.bfloat16))
        if keep < lines:
            slots.append(pltpu.VMEM((lines, width, width), jnp.bfloat16))
    vmem = pl.BlockSpec(memory_space=pltpu.VMEM)
    dma = pltpu.SemaphoreType.DMA
    square = pltpu.VMEM((width, width), jnp.float32)
    lower, solved = pl.pallas_call(
        functools.partial(kernel, nodes, levels, inner),
        out_shape=(square, square),
        in_specs=[pl.BlockSpec(memory_space=pltpu.SMEM), vmem, vmem],
        out_specs=(vmem, vmem),
        scratch_shapes=[
            pltpu.VMEM((width, 2 * width), jnp.float32),
            pltpu.VMEM((width, 2 * width), jnp.float32),
            pltpu.SMEM((nodes,), jnp.int32),
            pltpu.VMEM((steps, width, width), jnp.float32),
            pltpu.VMEM((steps, width, width), jnp.float32),
            pltpu.VMEM((steps, 2 * width, width), jnp.bfloat16),
            pltpu.VMEM((steps, 2 * width, width), jnp.bfloat16),
            dma((steps,)), dma((steps, HALVES, lines - 1)), dma((steps,)), dma((steps,)),
            dma((steps, 2)), dma((steps, 2)),
        ] + slots,
        compiler_params=pltpu.CompilerParams(collective_id=0, has_side_effects=True),
    )(targets.T, diag_blocks.reshape(width, width), panel_blocks.reshape(width, width))
    return lower[None], solved[None, None]


def solution(mesh):
    return jax.shard_map(
        shards,
        mesh=mesh,
        in_specs=(P("col", None, None), P("col", "grp", None, None), P()),
        out_specs=(P("col", None, None), P("col", "grp", None, None)),
        check_vma=False,
    )
```
